32 devices in a mesh: parts: 2 (over x), space: 16 (over z, y, core).
Axes of the slice: x: 2, y: 2, z: 4, core: 2. Of those that a mesh axis runs over, the one named last changes fastest.
Arguments:
- observed: bfloat16 [128, 4096, 128], P(('parts', 'space')), parts along dimension 0, may hold values from -6 to 6
- weights: bfloat16 [128, 4096, 128], P(('parts', 'space')), parts along dimension 0, may hold values from 0 to 1, as said below
- pixel_factors: float32 [128, 16, 4096], P(('parts', 'space')), parts along dimension 0, may hold values from -6 to 6
- pixel_bias: float32 [128, 4096], P(('parts', 'space')), parts along dimension 0, may hold values from -4 to 4
- date_factors: float32 [32, 128], P('parts'), parts along dimension 0, may hold values from -1.5 to 1.5
- date_bias: float32 [256], P('parts'), parts along dimension 0, may hold values from -4 to 4
- land_class: int32 [128, 4096], P(('parts', 'space')), parts along dimension 0, may hold values from 0 to 3
- conductance: float32 [4], replicated, may hold values from 0.3 to 3
Outputs:
- grad_pixel_factors: float32 [128, 16, 4096], P(('parts', 'space')), parts along dimension 0
- grad_pixel_bias: float32 [128, 4096], P(('parts', 'space')), parts along dimension 0
- grad_date_factors: float32 [32, 128], P('parts'), parts along dimension 0
- grad_date_bias: float32 [256], P('parts'), parts along dimension 0
The draws below stay inside these ranges and needn't reach their ends.
There are 2 independent parts, one for each index of `parts`. The reference program is written for one: setup_inputs(seed, part) draws one part's arguments, and reference() takes and returns one part's arrays. A program takes and returns all parts, laid end to end along the dimension named above; an argument that names none is the same for every part. Nothing has to cross between parts.
Inputs may be any that keep to these rules, and one draw needn't show every extreme that they name: Every pixel has a nonzero weight on at least one date; nonzero weights are 0.5 or more.
All inputs are finite; a program needn't handle non-finite values.
Results may differ from the reference program's by a relative error of at most 0.0003.
Values sent between devices are 32-bit elements; how exact they have to be, the bound alone decides.
A program may use at most 64 MiB of HBM per device.

```python
import math
import jax
import jax.numpy as jnp
from jax import lax

RANK = 16
COLS = 4096
DATES = 128
CLASSES = 4
ROWS = 64
PIXELS = 262144


def draw_weights(key, part):
    first, second, third = jax.random.split(jax.random.fold_in(key, 11), 3)
    position = jnp.arange(ROWS, dtype=jnp.float32) / max(ROWS - 1, 1)
    chance = 0.2 + 0.4 * position
    level = jax.random.uniform(third, (ROWS, COLS, DATES), jnp.float32, 0.5, 1.0)
    draws = jax.random.uniform(first, (ROWS, COLS, DATES), jnp.float32)
    forced = jax.random.randint(second, (ROWS, COLS, 1), 0, DATES)
    clear = (draws < chance[:, None, None]) | (jnp.arange(DATES)[None, None, :] == forced)
    return jnp.where(clear, level, jnp.float32(0.0)).astype(jnp.bfloat16)


def place_ends(array, stream_key, low, largest):
    longest = array.shape.index(max(array.shape))
    spots = []
    for shift in (0, 1):
        where = [jax.random.randint(jax.random.fold_in(stream_key, axis), (), 0, length) for axis, length in enumerate(array.shape)]
        where[longest] = (where[longest] + shift) % array.shape[longest]
        spots.append(tuple(where))
    return array.at[spots[0]].set(low).at[spots[1]].set(largest)


def block_levels(key, shape, pieces, smallest, high):
    def one(dim, parts):
        steps = jax.random.uniform(jax.random.fold_in(jax.random.fold_in(key, 6), dim), (parts,), jnp.float32, smallest / len(pieces), high / len(pieces))
        return jnp.repeat(jnp.exp(steps), shape[dim] // parts).reshape((-1,) + (1,) * (len(shape) - dim - 1))

    level = one(*pieces[0])
    for cut in pieces[1:]:
        level = level * one(*cut)
    return level


def gaussian(own_key, extent, spread, limit, cuts=(), held_as=jnp.bfloat16):
    loudness = block_levels(own_key, extent, cuts, -0.22, 0.18) if cuts else 1.0
    entries = jax.random.normal(own_key, extent, jnp.float32) * spread * loudness
    return jnp.minimum(jnp.maximum(entries, -limit), limit).astype(held_as)


def setup_inputs(seed: int = 0, part: int = 0) -> dict:
    seeds = jax.random.split(jax.random.key(seed), 9)
    part_keys = jax.random.split(jax.random.fold_in(seeds[8], part), 9)
    return {
        "observed": gaussian(part_keys[0], (ROWS, COLS, DATES), 1.0, 6.0, ((0, 16),)),
        "weights": draw_weights(jax.random.fold_in(jax.random.fold_in(seeds[8], part), 71), part),
        "pixel_factors": gaussian(part_keys[2], (ROWS, RANK, COLS), 1.0, 6.0, ((0, 16),), jnp.float32),
        "pixel_bias": gaussian(part_keys[3], (ROWS, COLS), 0.5, 4.0, ((0, 16),), jnp.float32),
        "date_factors": gaussian(part_keys[4], (RANK, DATES), RANK ** -0.5, 1.5, (), jnp.float32),
        "date_bias": gaussian(part_keys[5], (DATES,), 0.5, 4.0, (), jnp.float32),
        "land_class": place_ends(jax.random.randint(part_keys[6], (ROWS, COLS), 0, CLASSES), jax.random.fold_in(part_keys[6], 1), 0, CLASSES - 1).astype(jnp.int32),
        "conductance": jnp.clip(jnp.exp(jax.random.uniform(seeds[7], (CLASSES,), jnp.float32, math.log(0.3), math.log(3.0))), 0.3, 3.0),
    }


def lookup(land_class, conductance):
    cond = jnp.zeros(land_class.shape, jnp.float32)
    for klass in range(CLASSES):
        cond = cond + jnp.where(land_class == klass, conductance[klass], jnp.float32(0.0))
    return cond


def reference(observed, weights, pixel_factors, pixel_bias, date_factors, date_bias, land_class, conductance):
    count = jnp.sum(weights, dtype=jnp.float32)
    scale = jnp.float32(PIXELS) / count
    cond = lookup(land_class, conductance)
    weighted = cond[:, None, :] * pixel_factors
    stacked = jnp.concatenate([weighted, cond[:, None, :]], axis=1)
    padded = jnp.pad(stacked, ((1, 1), (0, 0), (1, 1)))
    beside_all = padded[:-2, :, 1:-1] + padded[2:, :, 1:-1] + padded[1:-1, :, :-2] + padded[1:-1, :, 2:]
    smooth = cond[:, None, :] * (beside_all[:, RANK:RANK + 1, :] * pixel_factors - beside_all[:, :RANK, :])
    block = math.gcd(ROWS, 16)
    blocks = ROWS // block
    hi = lax.Precision.HIGHEST

    def step(carry, items):
        obs, wts, fac, bias = items
        pred = jnp.einsum("yrw,rt->ywt", fac, date_factors, precision=hi) + bias[:, :, None] + date_bias
        resid = scale * wts.astype(jnp.float32) * (pred - obs.astype(jnp.float32))
        gfac = carry[0] + jnp.einsum("ywt,yrw->rt", resid, fac, precision=hi)
        gbias = carry[1] + jnp.sum(resid, axis=(0, 1))
        gpix = jnp.einsum("ywt,rt->yrw", resid, date_factors, precision=hi)
        return (gfac, gbias), (gpix, jnp.sum(resid, axis=2))

    items = (observed.reshape(blocks, block, COLS, DATES), weights.reshape(blocks, block, COLS, DATES),
             pixel_factors.reshape(blocks, block, RANK, COLS), pixel_bias.reshape(blocks, block, COLS))
    init = (jnp.zeros((RANK, DATES), jnp.float32), jnp.zeros((DATES,), jnp.float32))
    (gfac, gbias), (gpix, gpb) = lax.scan(step, init, items)
    grad_pixel_factors = gpix.reshape(ROWS, RANK, COLS) + smooth
    return grad_pixel_factors, gpb.reshape(ROWS, COLS), gfac, gbias
```

```python
import functools

import jax
import jax.numpy as jnp
from jax import lax
from jax.experimental import pallas as pl
from jax.experimental.pallas import tpu as pltpu
from jax.sharding import PartitionSpec as P

CLASSES = 4
CHUNK = 512
GRANT = 44 * 1024 * 1024


def split(x):
    head = x.astype(jnp.bfloat16)
    return head, (x - head.astype(jnp.float32)).astype(jnp.bfloat16)


def lookup(land_class, cond_ref):
    cond = jnp.zeros(land_class.shape, jnp.float32)
    for klass in range(CLASSES):
        cond = cond + jnp.where(land_class == klass, cond_ref[klass], jnp.float32(0.0))
    return cond


def beside(x):
    cols = x.shape[1]
    col = lax.broadcasted_iota(jnp.int32, x.shape, 1)
    left = jnp.where(col == 0, 0.0, pltpu.roll(x, 1, 1))
    right = jnp.where(col == cols - 1, 0.0, pltpu.roll(x, cols - 1, 1))
    return left + right


def kernel(
    n, chunk,
    cond_hbm, obs_hbm, wts_hbm, fac_hbm, pb_hbm, df_hbm, db_hbm, lc_hbm,
    gpf_ref, gpb_ref, gdf_ref, gdb_ref,
    cond_ref, df_ref, db_ref,
    obs, wts, fac, pb, lc, smooth, halo_f, halo_c, edge_c, rhs, back, misfits, parts, cond,
    obs_sem, wts_sem, fac_sem, small_sem,
    halo_send, halo_recv, part_sem, go_sem,
):
    rows, rank, cols = fac.shape
    dates = obs.shape[2]
    f32, bf16 = jnp.float32, jnp.bfloat16

    me = lax.axis_index("space")
    above, below = jnp.maximum(me - 1, 0), jnp.minimum(me + 1, n - 1)

    def signal(peer):
        pl.semaphore_signal(
            barrier, inc=1, device_id={"space": peer}, device_id_type=pl.DeviceIdType.MESH
        )

    def each_other(act):
        if n <= 32:
            for peer in range(1, n):
                act(peer)
        else:
            lax.fori_loop(1, n, lambda peer, none: (act(peer), none)[1], 0)

    barrier = pltpu.get_barrier_semaphore()
    is_root, is_last = me == 0, me == n - 1

    @pl.when(is_root)
    def _():
        each_other(signal)

    @pl.when(jnp.logical_not(is_root))
    def _():
        signal(0)

        @pl.when(me > 1)
        def _():
            signal(above)

        @pl.when(jnp.logical_not(is_last))
        def _():
            signal(below)

    df_copy = pltpu.make_async_copy(df_hbm, df_ref, small_sem.at[2])
    db_copy = pltpu.make_async_copy(db_hbm, db_ref, small_sem.at[3])
    cond_copy = pltpu.make_async_copy(cond_hbm, cond_ref, small_sem.at[4])
    pb_copy = pltpu.make_async_copy(pb_hbm, pb, small_sem.at[0])
    lc_copy = pltpu.make_async_copy(lc_hbm, lc, small_sem.at[1])
    fac_copies = [
        pltpu.make_async_copy(fac_hbm.at[y], fac.at[y], fac_sem.at[y]) for y in range(rows)
    ]
    obs_copies = [
        pltpu.make_async_copy(obs_hbm.at[y], obs.at[y], obs_sem.at[y]) for y in range(rows)
    ]
    wts_copies = [
        pltpu.make_async_copy(wts_hbm.at[y], wts.at[y], wts_sem.at[y]) for y in range(rows)
    ]
    cond_copy.start()
    lc_copy.start()
    df_copy.start()
    db_copy.start()
    pb_copy.start()
    for y in range(rows):
        for copies in (fac_copies, wts_copies, obs_copies):
            copies[y].start()

    df_copy.wait()
    db_copy.wait()
    dh, dl = split(df_ref[...])
    bh, bl = split(db_ref[...])
    line = lax.broadcasted_iota(jnp.int32, (16, dates), 0)
    tail = jnp.where(
        line < 2, 1.0,
        jnp.where(line == 2, bh.astype(f32), jnp.where(line == 3, bl.astype(f32), 0.0)),
    ).astype(bf16)
    one = jnp.concatenate([dh, dh, dl, tail], axis=0)
    none = jnp.zeros_like(one)
    rhs[...] = jnp.concatenate(
        [jnp.concatenate([one, none], axis=1), jnp.concatenate([none, one], axis=1)], axis=0
    )
    ones_line = jnp.where(line == 0, 1.0, 0.0).astype(bf16)
    back[...] = jnp.concatenate(
        [
            jnp.concatenate([dh, dh], axis=1),
            jnp.concatenate([dl, jnp.zeros_like(dl)], axis=1),
            jnp.concatenate([ones_line, ones_line], axis=1),
        ],
        axis=0,
    )

    def remote(src, dst, send, recv, peer):
        return pltpu.make_async_remote_copy(
            src_ref=src, dst_ref=dst, send_sem=send, recv_sem=recv,
            device_id={"space": peer}, device_id_type=pl.DeviceIdType.MESH,
        )

    def wait_bytes(ref, sem):
        pltpu.make_async_copy(ref, ref, sem).wait()

    halo = [
        remote(fac_hbm.at[0], halo_f.at[1], halo_send.at[0], halo_recv.at[0], above),
        remote(fac_hbm.at[rows - 1], halo_f.at[0], halo_send.at[1], halo_recv.at[1], below),
        remote(edge_c.at[0], halo_c.at[1], halo_send.at[2], halo_recv.at[2], above),
        remote(edge_c.at[1], halo_c.at[0], halo_send.at[3], halo_recv.at[3], below),
    ]
    pb_copy.wait()

    def greet():
        lc_copy.wait()
        cond_copy.wait()
        cond[1 : rows + 1] = lookup(lc[...], cond_ref)
        edge_c[0] = cond[1:2]
        edge_c[1] = cond[rows : rows + 1]


        @pl.when(jnp.logical_not(is_root))
        def _():
            halo[0].start()
            halo[2].start()

        @pl.when(jnp.logical_not(is_last))
        def _():
            halo[1].start()
            halo[3].start()

    slot = lax.broadcasted_iota(jnp.int32, (16, chunk), 0)

    def operand(y, start):
        at = pl.ds(start, chunk)
        fh, fl = split(fac[y, :, at])
        ph, plow = split(pb[pl.ds(y, 1), at])
        extra = jnp.where(
            slot == 0, ph.astype(f32),
            jnp.where(slot == 1, plow.astype(f32), jnp.where(slot < 4, 1.0, 0.0)),
        ).astype(bf16)
        return jnp.concatenate([fh, fl, fh, extra], axis=0)

    def forward(y, carry):
        total, count = carry
        for copies in (fac_sem, fac), (wts_sem, wts), (obs_sem, obs):
            pltpu.make_async_copy(copies[1].at[y], copies[1].at[y], copies[0].at[y]).wait()
        half = cols // 2
        for start in range(0, half, chunk):
            lhs = [operand(y, start), operand(y, half + start)]
            pred = lax.dot_general(
                jnp.concatenate(lhs, axis=0), rhs[...], (((0,), (0,)), ((), ())),
                preferred_element_type=f32,
            )
            for j in range(2):
                at = pl.ds(j * half + start, chunk)
                w = wts[y, at].astype(f32)
                count = count + jnp.sum(w.reshape(chunk // 8, 8, dates), axis=0)
                misfit = w * (pred[:, j * dates : (j + 1) * dates] - obs[y, at].astype(f32))
                mh, ml = split(misfit)
                both = jnp.concatenate([mh, ml], axis=1)
                misfits[y, at] = both
                total = total + lax.dot_general(
                    lhs[j], both, (((1,), (0,)), ((), ())), preferred_element_type=f32
                )
        return total, count

    carry = (jnp.zeros((64, 2 * dates), f32), jnp.zeros((8, dates), f32))

    @pl.when(jnp.logical_not(is_root))
    def _():
        pl.semaphore_wait(
            barrier, 3 - (me == 1).astype(jnp.int32) - is_last.astype(jnp.int32)
        )
        greet()
    total, count = lax.fori_loop(0, rows, forward, carry)

    gdf = total[:rank, :dates] + total[:rank, dates:] + total[rank : 2 * rank, :dates]
    gdb = total[50:51, :dates] + total[50:51, dates:]
    parts[me] = jnp.concatenate(
        [gdf, gdb, jnp.sum(count, axis=0, keepdims=True), jnp.zeros((6, dates), f32)], axis=0
    )

    def send_part(peer):
        remote(parts.at[me], parts.at[me], part_sem.at[0], part_sem.at[1], peer).start()

    @pl.when(jnp.logical_not(is_root))
    def _():
        send_part(0)
        pl.semaphore_wait(go_sem, 1)
        for k in range(1, n) if n <= 32 else ():
            peer = lax.rem(me + k, n)

            @pl.when(peer > 0)
            def _():
                send_part(peer)

        if n > 32:

            def step(k, none):
                peer = lax.rem(me + k, n)

                @pl.when(peer > 0)
                def _():
                    send_part(peer)

                return none

            lax.fori_loop(1, n, step, 0)

    @pl.when(is_root)
    def _():
        pl.semaphore_wait(barrier, n - 1)
        each_other(
            lambda peer: pl.semaphore_signal(
                go_sem, inc=1, device_id={"space": peer}, device_id_type=pl.DeviceIdType.MESH
            )
        )
        greet()
        each_other(send_part)


    def backward(y, none):
        pix = lax.dot_general(
            back[...], misfits[y], (((1,), (1,)), ((), ())), preferred_element_type=f32
        )
        gpf_ref[y] = pix[:rank] + pix[rank : 2 * rank]
        gpb_ref[pl.ds(y, 1)] = pix[2 * rank : 2 * rank + 1]
        return none

    lax.fori_loop(0, rows, backward, 0)

    def row_factors(y):
        return halo_f[0] if y < 0 else halo_f[1] if y == rows else fac[y]

    def smooth_row(y):
        own = cond[y + 1 : y + 2]
        north, south = cond[y : y + 1], cond[y + 2 : y + 3]
        f = fac[y]
        around = north + south + beside(own)
        weighted = north * row_factors(y - 1) + south * row_factors(y + 1) + beside(own * f)
        smooth[y] = own * (around * f - weighted)

    for y in range(1, rows - 1):
        smooth_row(y)

    @pl.when(is_root)
    def _():
        halo_f[0] = jnp.zeros((rank, cols), f32)
        halo_c[0] = jnp.zeros((1, cols), f32)

    @pl.when(jnp.logical_not(is_root))
    def _():
        halo[0].wait_send()
        halo[2].wait_send()
        halo[1].wait_recv()
        halo[3].wait_recv()

    @pl.when(is_last)
    def _():
        halo_f[1] = jnp.zeros((rank, cols), f32)
        halo_c[1] = jnp.zeros((1, cols), f32)

    @pl.when(jnp.logical_not(is_last))
    def _():
        halo[1].wait_send()
        halo[3].wait_send()
        halo[0].wait_recv()
        halo[2].wait_recv()

    cond[0:1] = halo_c[0]
    cond[rows + 1 : rows + 2] = halo_c[1]
    smooth_row(0)
    smooth_row(rows - 1)


    others = parts.at[pl.ds(0, n - 1)]
    wait_bytes(others, part_sem.at[1])
    whole = jnp.sum(parts[...], axis=0)
    clear = jnp.sum(whole[rank + 1 : rank + 2], axis=1, keepdims=True)
    scale = jnp.float32(n * rows * cols) / clear
    gdf_ref[...] = scale * whole[:rank]
    gdb_ref[...] = scale * whole[rank : rank + 1]
    gpb_ref[...] = scale * gpb_ref[...]
    for y in range(rows):
        gpf_ref[y] = scale * gpf_ref[y] + smooth[y]
    wait_bytes(others, part_sem.at[0])


def place(*refs):
    half = len(refs) // 2
    sem = refs[-1]
    copies = [
        pltpu.make_async_copy(refs[i], refs[half + i], sem.at[i]) for i in range(half)
    ]
    for copy in copies:
        copy.start()
    for copy in copies:
        copy.wait()


def on_device(
    observed, weights, pixel_factors, pixel_bias, date_factors, date_bias, land_class, conductance
):
    rows, rank, cols = pixel_factors.shape
    dates = observed.shape[2]
    n = lax.axis_size("space")
    f32, bf16 = jnp.float32, jnp.bfloat16
    dma = pltpu.SemaphoreType.DMA
    anywhere = pl.BlockSpec(memory_space=pl.ANY)
    vmem = pl.BlockSpec(memory_space=pltpu.VMEM)
    shapes = (
        jax.ShapeDtypeStruct((rows, rank, cols), f32),
        jax.ShapeDtypeStruct((rows, cols), f32),
        jax.ShapeDtypeStruct((rank, dates), f32),
        jax.ShapeDtypeStruct((1, dates), f32),
    )
    grads = pl.pallas_call(
        functools.partial(kernel, n, min(CHUNK, cols // 2)),
        out_shape=tuple(pltpu.VMEM(x.shape, x.dtype) for x in shapes),
        in_specs=[anywhere] * 8,
        out_specs=(vmem,) * 4,
        scratch_shapes=[
            pltpu.SMEM((CLASSES,), f32),
            pltpu.VMEM((rank, dates), f32),
            pltpu.VMEM((1, dates), f32),
            pltpu.VMEM((rows, cols, dates), bf16),
            pltpu.VMEM((rows, cols, dates), bf16),
            pltpu.VMEM((rows, rank, cols), f32),
            pltpu.VMEM((rows, cols), f32),
            pltpu.VMEM((rows, cols), jnp.int32),
            pltpu.VMEM((rows, rank, cols), f32),
            pltpu.VMEM((2, rank, cols), f32),
            pltpu.VMEM((2, 1, cols), f32),
            pltpu.VMEM((2, 1, cols), f32),
            pltpu.VMEM((128, 2 * dates), bf16),
            pltpu.VMEM((48, 2 * dates), bf16),
            pltpu.VMEM((rows, cols, 2 * dates), bf16),
            pltpu.VMEM((n, 24, dates), f32),
            pltpu.VMEM((rows + 2, cols), f32),
            dma((rows,)), dma((rows,)), dma((rows,)), dma((5,)),
            dma((4,)), dma((4,)), dma((2,)),
            pltpu.SemaphoreType.REGULAR,
        ],
        compiler_params=pltpu.CompilerParams(
            collective_id=0, has_side_effects=True, vmem_limit_bytes=GRANT
        ),
        name="gap_fill",
    )(
        *(
            pltpu.with_memory_space_constraint(x, pltpu.HBM)
            for x in (
                conductance, observed, weights, pixel_factors, pixel_bias, date_factors,
                date_bias.reshape(1, dates), land_class,
            )
        )
    )
    gpf, gpb, gdf, gdb = pl.pallas_call(
        place,
        out_shape=shapes,
        in_specs=[vmem] * 4,
        out_specs=(anywhere,) * 4,
        scratch_shapes=[dma((4,))],
        compiler_params=pltpu.CompilerParams(vmem_limit_bytes=4 * 1024 * 1024),
        name="place",
    )(*grads)
    return gpf, gpb, gdf, gdb.reshape(dates)


def solution(mesh):
    return jax.shard_map(
        on_device,
        mesh=mesh,
        in_specs=(
            P(("parts", "space"), None, None),
            P(("parts", "space"), None, None),
            P(("parts", "space"), None, None),
            P(("parts", "space"), None),
            P("parts", None),
            P("parts"),
            P(("parts", "space"), None),
            P(),
        ),
        out_specs=(
            P(("parts", "space"), None, None),
            P(("parts", "space"), None),
            P("parts", None),
            P("parts"),
        ),
        check_vma=False,
    )
```

```python
import functools

import jax
import jax.numpy as jnp
from jax import lax
from jax.experimental import pallas as pl
from jax.experimental.pallas import tpu as pltpu
from jax.sharding import PartitionSpec as P

CLASSES = 4
CHUNK = 256
GRANT = 44 * 1024 * 1024


def split(x):
    head = x.astype(jnp.bfloat16)
    return head, (x - head.astype(jnp.float32)).astype(jnp.bfloat16)


def lookup(land_class, cond_ref):
    cond = jnp.zeros(land_class.shape, jnp.float32)
    for klass in range(CLASSES):
        cond = cond + jnp.where(land_class == klass, cond_ref[klass], jnp.float32(0.0))
    return cond


def beside(x):
    cols = x.shape[1]
    col = lax.broadcasted_iota(jnp.int32, x.shape, 1)
    left = jnp.where(col == 0, 0.0, pltpu.roll(x, 1, 1))
    right = jnp.where(col == cols - 1, 0.0, pltpu.roll(x, cols - 1, 1))
    return left + right


def kernel(
    n, chunk,
    cond_hbm, obs_hbm, wts_hbm, fac_hbm, pb_hbm, df_hbm, db_hbm, lc_hbm,
    gpf_ref, gpb_ref, gdf_ref, gdb_ref,
    cond_ref, df_ref, db_ref,
    obs, wts, fac, pb, lc, smooth, halo_f, halo_c, edge_c, rhs, back, misfits, parts, cond,
    obs_sem, wts_sem, fac_sem, small_sem,
    halo_send, halo_recv, part_sem, go_sem,
):
    rows, rank, cols = fac.shape
    dates = obs.shape[2]
    f32, bf16 = jnp.float32, jnp.bfloat16

    me = lax.axis_index("space")
    above, below = jnp.maximum(me - 1, 0), jnp.minimum(me + 1, n - 1)

    def signal(peer):
        pl.semaphore_signal(
            barrier, inc=1, device_id={"space": peer}, device_id_type=pl.DeviceIdType.MESH
        )

    def each_other(act):
        if n <= 32:
            for peer in range(1, n):
                act(peer)
        else:
            lax.fori_loop(1, n, lambda peer, none: (act(peer), none)[1], 0)

    barrier = pltpu.get_barrier_semaphore()
    is_root, is_last = me == 0, me == n - 1

    @pl.when(is_root)
    def _():
        each_other(signal)

    @pl.when(jnp.logical_not(is_root))
    def _():
        signal(0)

        @pl.when(me > 1)
        def _():
            signal(above)

        @pl.when(jnp.logical_not(is_last))
        def _():
            signal(below)

    df_copy = pltpu.make_async_copy(df_hbm, df_ref, small_sem.at[2])
    db_copy = pltpu.make_async_copy(db_hbm, db_ref, small_sem.at[3])
    cond_copy = pltpu.make_async_copy(cond_hbm, cond_ref, small_sem.at[4])
    pb_copy = pltpu.make_async_copy(pb_hbm, pb, small_sem.at[0])
    lc_copy = pltpu.make_async_copy(lc_hbm, lc, small_sem.at[1])
    fac_copies = [
        pltpu.make_async_copy(fac_hbm.at[y], fac.at[y], fac_sem.at[y]) for y in range(rows)
    ]
    obs_copies = [
        pltpu.make_async_copy(obs_hbm.at[y], obs.at[y], obs_sem.at[y]) for y in range(rows)
    ]
    wts_copies = [
        pltpu.make_async_copy(wts_hbm.at[y], wts.at[y], wts_sem.at[y]) for y in range(rows)
    ]
    cond_copy.start()
    lc_copy.start()
    df_copy.start()
    db_copy.start()
    pb_copy.start()
    for copy in fac_copies:
        copy.start()
    wts_copies[0].start()
    obs_copies[0].start()

    df_copy.wait()
    db_copy.wait()
    dh, dl = split(df_ref[...])
    bh, bl = split(db_ref[...])
    line = lax.broadcasted_iota(jnp.int32, (16, dates), 0)
    tail = jnp.where(
        line < 2, 1.0,
        jnp.where(line == 2, bh.astype(f32), jnp.where(line == 3, bl.astype(f32), 0.0)),
    ).astype(bf16)
    one = jnp.concatenate([dh, dh, dl, tail], axis=0)
    none = jnp.zeros_like(one)
    rhs[...] = jnp.concatenate(
        [jnp.concatenate([one, none], axis=1), jnp.concatenate([none, one], axis=1)], axis=0
    )
    ones_line = jnp.where(line == 0, 1.0, 0.0).astype(bf16)
    back[...] = jnp.concatenate(
        [
            jnp.concatenate([dh, dh], axis=1),
            jnp.concatenate([dl, jnp.zeros_like(dl)], axis=1),
            jnp.concatenate([ones_line, ones_line], axis=1),
        ],
        axis=0,
    )

    def remote(src, dst, send, recv, peer):
        return pltpu.make_async_remote_copy(
            src_ref=src, dst_ref=dst, send_sem=send, recv_sem=recv,
            device_id={"space": peer}, device_id_type=pl.DeviceIdType.MESH,
        )

    def wait_bytes(ref, sem):
        pltpu.make_async_copy(ref, ref, sem).wait()

    halo = [
        remote(fac_hbm.at[0], halo_f.at[1], halo_send.at[0], halo_recv.at[0], above),
        remote(fac_hbm.at[rows - 1], halo_f.at[0], halo_send.at[1], halo_recv.at[1], below),
        remote(edge_c.at[0], halo_c.at[1], halo_send.at[2], halo_recv.at[2], above),
        remote(edge_c.at[1], halo_c.at[0], halo_send.at[3], halo_recv.at[3], below),
    ]
    pb_copy.wait()

    def greet():
        lc_copy.wait()
        cond_copy.wait()
        cond[1 : rows + 1] = lookup(lc[...], cond_ref)
        edge_c[0] = cond[1:2]
        edge_c[1] = cond[rows : rows + 1]


        @pl.when(jnp.logical_not(is_root))
        def _():
            halo[0].start()
            halo[2].start()

        @pl.when(jnp.logical_not(is_last))
        def _():
            halo[1].start()
            halo[3].start()

    slot = lax.broadcasted_iota(jnp.int32, (16, chunk), 0)

    def operand(y, start):
        at = pl.ds(start, chunk)
        fh, fl = split(fac[y, :, at])
        ph, plow = split(pb[y : y + 1, at])
        extra = jnp.where(
            slot == 0, ph.astype(f32),
            jnp.where(slot == 1, plow.astype(f32), jnp.where(slot < 4, 1.0, 0.0)),
        ).astype(bf16)
        return jnp.concatenate([fh, fl, fh, extra], axis=0)

    wts_copies[1].start()
    obs_copies[1].start()

    @pl.when(jnp.logical_not(is_root))
    def _():
        pl.semaphore_wait(
            barrier, 3 - (me == 1).astype(jnp.int32) - is_last.astype(jnp.int32)
        )
        greet()

    blocks = cols // (2 * chunk)
    for copy in fac_copies:
        copy.wait()
    def predict(y, b):
        start = b * 2 * chunk
        lhs = [operand(y, start), operand(y, start + chunk)]
        pred = lax.dot_general(
            jnp.concatenate(lhs, axis=0), rhs[...], (((0,), (0,)), ((), ())),
            preferred_element_type=f32,
        )
        return lhs, pred

    def misfit_of(y, b, pred):
        pieces, weight = [], None
        for j in range(2):
            at = pl.ds((2 * b + j) * chunk, chunk)
            w = wts[y, at].astype(f32)
            own = jnp.sum(w.reshape(chunk // 8, 8, dates), axis=0)
            weight = own if weight is None else weight + own
            mh, ml = split(w * (pred[:, j * dates : (j + 1) * dates] - obs[y, at].astype(f32)))
            both = jnp.concatenate([mh, ml], axis=1)
            misfits[y, at] = both
            pieces.append(both)
        return pieces, weight

    def gather(lhs, pieces):
        return sum(
            lax.dot_general(
                lhs[j], pieces[j], (((1,), (0,)), ((), ())), preferred_element_type=f32
            )
            for j in range(2)
        )

    total = jnp.zeros((64, 2 * dates), f32)
    count = jnp.zeros((8, dates), f32)
    predicted = ready = None
    for step in range(rows * blocks + 2):
        y, b = divmod(step, blocks)
        if y < rows and b == 0:
            wts_copies[y].wait()
            obs_copies[y].wait()
            if y + 2 < rows:
                wts_copies[y + 2].start()
                obs_copies[y + 2].start()
        now = (y, b, *predict(y, b)) if y < rows else None
        if ready is not None:
            total = total + gather(*ready)
        ready = None
        if predicted is not None:
            py, pb_, lhs, pred = predicted
            pieces, weight = misfit_of(py, pb_, pred)
            count = count + weight
            ready = lhs, pieces
        predicted = now

    gdf = total[:rank, :dates] + total[:rank, dates:] + total[rank : 2 * rank, :dates]
    gdb = total[50:51, :dates] + total[50:51, dates:]
    parts[me] = jnp.concatenate(
        [gdf, gdb, jnp.sum(count, axis=0, keepdims=True), jnp.zeros((6, dates), f32)], axis=0
    )

    def send_part(peer):
        remote(parts.at[me], parts.at[me], part_sem.at[0], part_sem.at[1], peer).start()

    @pl.when(jnp.logical_not(is_root))
    def _():
        send_part(0)
        pl.semaphore_wait(go_sem, 1)
        for k in range(1, n) if n <= 32 else ():
            peer = lax.rem(me + k, n)

            @pl.when(peer > 0)
            def _():
                send_part(peer)

        if n > 32:

            def step(k, none):
                peer = lax.rem(me + k, n)

                @pl.when(peer > 0)
                def _():
                    send_part(peer)

                return none

            lax.fori_loop(1, n, step, 0)

    @pl.when(is_root)
    def _():
        pl.semaphore_wait(barrier, n - 1)
        each_other(
            lambda peer: pl.semaphore_signal(
                go_sem, inc=1, device_id={"space": peer}, device_id_type=pl.DeviceIdType.MESH
            )
        )
        greet()
        each_other(send_part)


    for y in range(rows):
        pix = lax.dot_general(
            back[...], misfits[y], (((1,), (1,)), ((), ())), preferred_element_type=f32
        )
        gpf_ref[y] = pix[:rank] + pix[rank : 2 * rank]
        gpb_ref[y : y + 1] = pix[2 * rank : 2 * rank + 1]

    def row_factors(y):
        return halo_f[0] if y < 0 else halo_f[1] if y == rows else fac[y]

    def smooth_row(y):
        own = cond[y + 1 : y + 2]
        north, south = cond[y : y + 1], cond[y + 2 : y + 3]
        f = fac[y]
        around = north + south + beside(own)
        weighted = north * row_factors(y - 1) + south * row_factors(y + 1) + beside(own * f)
        smooth[y] = own * (around * f - weighted)

    for y in range(1, rows - 1):
        smooth_row(y)

    @pl.when(is_root)
    def _():
        halo_f[0] = jnp.zeros((rank, cols), f32)
        halo_c[0] = jnp.zeros((1, cols), f32)

    @pl.when(jnp.logical_not(is_root))
    def _():
        halo[0].wait_send()
        halo[2].wait_send()
        halo[1].wait_recv()
        halo[3].wait_recv()

    @pl.when(is_last)
    def _():
        halo_f[1] = jnp.zeros((rank, cols), f32)
        halo_c[1] = jnp.zeros((1, cols), f32)

    @pl.when(jnp.logical_not(is_last))
    def _():
        halo[1].wait_send()
        halo[3].wait_send()
        halo[0].wait_recv()
        halo[2].wait_recv()

    cond[0:1] = halo_c[0]
    cond[rows + 1 : rows + 2] = halo_c[1]
    smooth_row(0)
    smooth_row(rows - 1)


    others = parts.at[pl.ds(0, n - 1)]
    wait_bytes(others, part_sem.at[1])
    whole = jnp.sum(parts[...], axis=0)
    clear = jnp.sum(whole[rank + 1 : rank + 2], axis=1, keepdims=True)
    scale = jnp.float32(n * rows * cols) / clear
    gdf_ref[...] = scale * whole[:rank]
    gdb_ref[...] = scale * whole[rank : rank + 1]
    gpb_ref[...] = scale * gpb_ref[...]
    for y in range(rows):
        gpf_ref[y] = scale * gpf_ref[y] + smooth[y]
    wait_bytes(others, part_sem.at[0])


def place(*refs):
    half = len(refs) // 2
    sem = refs[-1]
    copies = [
        pltpu.make_async_copy(refs[i], refs[half + i], sem.at[i]) for i in range(half)
    ]
    for copy in copies:
        copy.start()
    for copy in copies:
        copy.wait()


def on_device(
    observed, weights, pixel_factors, pixel_bias, date_factors, date_bias, land_class, conductance
):
    rows, rank, cols = pixel_factors.shape
    dates = observed.shape[2]
    n = lax.axis_size("space")
    f32, bf16 = jnp.float32, jnp.bfloat16
    dma = pltpu.SemaphoreType.DMA
    anywhere = pl.BlockSpec(memory_space=pl.ANY)
    vmem = pl.BlockSpec(memory_space=pltpu.VMEM)
    shapes = (
        jax.ShapeDtypeStruct((rows, rank, cols), f32),
        jax.ShapeDtypeStruct((rows, cols), f32),
        jax.ShapeDtypeStruct((rank, dates), f32),
        jax.ShapeDtypeStruct((1, dates), f32),
    )
    grads = pl.pallas_call(
        functools.partial(kernel, n, CHUNK),
        out_shape=tuple(pltpu.VMEM(x.shape, x.dtype) for x in shapes),
        in_specs=[anywhere] * 8,
        out_specs=(vmem,) * 4,
        scratch_shapes=[
            pltpu.SMEM((CLASSES,), f32),
            pltpu.VMEM((rank, dates), f32),
            pltpu.VMEM((1, dates), f32),
            pltpu.VMEM((rows, cols, dates), bf16),
            pltpu.VMEM((rows, cols, dates), bf16),
            pltpu.VMEM((rows, rank, cols), f32),
            pltpu.VMEM((rows, cols), f32),
            pltpu.VMEM((rows, cols), jnp.int32),
            pltpu.VMEM((rows, rank, cols), f32),
            pltpu.VMEM((2, rank, cols), f32),
            pltpu.VMEM((2, 1, cols), f32),
            pltpu.VMEM((2, 1, cols), f32),
            pltpu.VMEM((128, 2 * dates), bf16),
            pltpu.VMEM((48, 2 * dates), bf16),
            pltpu.VMEM((rows, cols, 2 * dates), bf16),
            pltpu.VMEM((n, 24, dates), f32),
            pltpu.VMEM((rows + 2, cols), f32),
            dma((rows,)), dma((rows,)), dma((rows,)), dma((5,)),
            dma((4,)), dma((4,)), dma((2,)),
            pltpu.SemaphoreType.REGULAR,
        ],
        compiler_params=pltpu.CompilerParams(
            collective_id=0, has_side_effects=True, vmem_limit_bytes=GRANT
        ),
        name="gap_fill",
    )(
        *(
            pltpu.with_memory_space_constraint(x, pltpu.HBM)
            for x in (
                conductance, observed, weights, pixel_factors, pixel_bias, date_factors,
                date_bias.reshape(1, dates), land_class,
            )
        )
    )
    gpf, gpb, gdf, gdb = pl.pallas_call(
        place,
        out_shape=shapes,
        in_specs=[vmem] * 4,
        out_specs=(anywhere,) * 4,
        scratch_shapes=[dma((4,))],
        compiler_params=pltpu.CompilerParams(vmem_limit_bytes=4 * 1024 * 1024),
        name="place",
    )(*grads)
    return gpf, gpb, gdf, gdb.reshape(dates)


def solution(mesh):
    return jax.shard_map(
        on_device,
        mesh=mesh,
        in_specs=(
            P(("parts", "space"), None, None),
            P(("parts", "space"), None, None),
            P(("parts", "space"), None, None),
            P(("parts", "space"), None),
            P("parts", None),
            P("parts"),
            P(("parts", "space"), None),
            P(),
        ),
        out_specs=(
            P(("parts", "space"), None, None),
            P(("parts", "space"), None),
            P("parts", None),
            P("parts"),
        ),
        check_vma=False,
    )
```

```python
import functools

import jax
import jax.numpy as jnp
from jax import lax
from jax.experimental import pallas as pl
from jax.experimental.pallas import tpu as pltpu
from jax.sharding import PartitionSpec as P

CLASSES = 4
CHUNK = 256
GRANT = 44 * 1024 * 1024


def split(x):
    head = x.astype(jnp.bfloat16)
    return head, (x - head.astype(jnp.float32)).astype(jnp.bfloat16)


def lookup(land_class, cond_ref):
    cond = jnp.zeros(land_class.shape, jnp.float32)
    for klass in range(CLASSES):
        cond = cond + jnp.where(land_class == klass, cond_ref[klass], jnp.float32(0.0))
    return cond


def beside(x):
    cols = x.shape[1]
    col = lax.broadcasted_iota(jnp.int32, x.shape, 1)
    left = jnp.where(col == 0, 0.0, pltpu.roll(x, 1, 1))
    right = jnp.where(col == cols - 1, 0.0, pltpu.roll(x, cols - 1, 1))
    return left + right


def kernel(
    n, chunk,
    cond_hbm, obs_hbm, wts_hbm, fac_hbm, pb_hbm, df_hbm, db_hbm, lc_hbm,
    gpf_ref, gpb_ref, gdf_ref, gdb_ref,
    cond_ref, df_ref, db_ref,
    obs, wts, fac, pb, lc, smooth, halo_f, halo_c, edge_c, rhs, back, misfits, parts, cond,
    obs_sem, wts_sem, fac_sem, small_sem,
    halo_send, halo_recv, part_sem, go_sem,
):
    rows, rank, cols = fac.shape
    dates = obs.shape[2]
    f32, bf16 = jnp.float32, jnp.bfloat16

    me = lax.axis_index("space")
    above, below = jnp.maximum(me - 1, 0), jnp.minimum(me + 1, n - 1)

    def signal(peer):
        pl.semaphore_signal(
            barrier, inc=1, device_id={"space": peer}, device_id_type=pl.DeviceIdType.MESH
        )

    def each_other(act):
        if n <= 32:
            for peer in range(1, n):
                act(peer)
        else:
            lax.fori_loop(1, n, lambda peer, none: (act(peer), none)[1], 0)

    barrier = pltpu.get_barrier_semaphore()
    is_root, is_last = me == 0, me == n - 1

    df_copy = pltpu.make_async_copy(df_hbm, df_ref, small_sem.at[2])
    db_copy = pltpu.make_async_copy(db_hbm, db_ref, small_sem.at[3])
    cond_copy = pltpu.make_async_copy(cond_hbm, cond_ref, small_sem.at[4])
    pb_copy = pltpu.make_async_copy(pb_hbm, pb, small_sem.at[0])
    lc_copy = pltpu.make_async_copy(lc_hbm, lc, small_sem.at[1])
    fac_copies = [
        pltpu.make_async_copy(fac_hbm.at[y], fac.at[y], fac_sem.at[y]) for y in range(rows)
    ]
    obs_copies = [
        pltpu.make_async_copy(obs_hbm.at[y], obs.at[y], obs_sem.at[y]) for y in range(rows)
    ]
    wts_copies = [
        pltpu.make_async_copy(wts_hbm.at[y], wts.at[y], wts_sem.at[y]) for y in range(rows)
    ]
    cond_copy.start()
    lc_copy.start()
    df_copy.start()
    db_copy.start()
    pb_copy.start()
    groups = [[0], [1], [2], [3]]

    def fetch(g):
        if g < len(groups):
            for y in groups[g]:
                fac_copies[y].start()
                wts_copies[y].start()
                obs_copies[y].start()

    for g in range(1):
        fetch(g)

    @pl.when(is_root)
    def _():
        each_other(signal)

    @pl.when(jnp.logical_not(is_root))
    def _():
        signal(0)

        @pl.when(me > 1)
        def _():
            signal(above)

        @pl.when(jnp.logical_not(is_last))
        def _():
            signal(below)

    df_copy.wait()
    db_copy.wait()
    dh, dl = split(df_ref[...])
    bh, bl = split(db_ref[...])
    line = lax.broadcasted_iota(jnp.int32, (16, dates), 0)
    tail = jnp.where(
        line < 2, 1.0,
        jnp.where(line == 2, bh.astype(f32), jnp.where(line == 3, bl.astype(f32), 0.0)),
    ).astype(bf16)
    one = jnp.concatenate([dh, dh, tail, dl], axis=0)
    none = jnp.zeros_like(one)
    rhs[...] = jnp.concatenate(
        [jnp.concatenate([one, none], axis=1), jnp.concatenate([none, one], axis=1)], axis=0
    )
    ones_line = jnp.where(line == 0, 1.0, 0.0).astype(bf16)
    back[...] = jnp.concatenate(
        [
            jnp.concatenate([dh, dh], axis=1),
            jnp.concatenate([dl, jnp.zeros_like(dl)], axis=1),
            jnp.concatenate([ones_line, ones_line], axis=1),
        ],
        axis=0,
    )

    def remote(src, dst, send, recv, peer):
        return pltpu.make_async_remote_copy(
            src_ref=src, dst_ref=dst, send_sem=send, recv_sem=recv,
            device_id={"space": peer}, device_id_type=pl.DeviceIdType.MESH,
        )

    def wait_bytes(ref, sem):
        pltpu.make_async_copy(ref, ref, sem).wait()

    halo = [
        remote(fac_hbm.at[0], halo_f.at[1], halo_send.at[0], halo_recv.at[0], above),
        remote(fac_hbm.at[rows - 1], halo_f.at[0], halo_send.at[1], halo_recv.at[1], below),
        remote(edge_c.at[0], halo_c.at[1], halo_send.at[2], halo_recv.at[2], above),
        remote(edge_c.at[1], halo_c.at[0], halo_send.at[3], halo_recv.at[3], below),
    ]
    pb_copy.wait()

    def greet():
        lc_copy.wait()
        cond_copy.wait()
        cond[1 : rows + 1] = lookup(lc[...], cond_ref)
        edge_c[0] = cond[1:2]
        edge_c[1] = cond[rows : rows + 1]


        @pl.when(jnp.logical_not(is_root))
        def _():
            halo[0].start()
            halo[2].start()

        @pl.when(jnp.logical_not(is_last))
        def _():
            halo[1].start()
            halo[3].start()

    slot = lax.broadcasted_iota(jnp.int32, (16, chunk), 0)

    def operand(y, start):
        at = pl.ds(start, chunk)
        fh, fl = split(fac[y, :, at])
        ph, plow = split(pb[y : y + 1, at])
        extra = jnp.where(
            slot == 0, ph.astype(f32),
            jnp.where(slot == 1, plow.astype(f32), jnp.where(slot < 4, 1.0, 0.0)),
        ).astype(bf16)
        return jnp.concatenate([fh, fl, extra, fh], axis=0)

    for g in range(1, 2):
        fetch(g)

    @pl.when(jnp.logical_not(is_root))
    def _():
        pl.semaphore_wait(
            barrier, 3 - (me == 1).astype(jnp.int32) - is_last.astype(jnp.int32)
        )
        greet()

    blocks = cols // (2 * chunk)
    def predict(y, b):
        start = b * 2 * chunk
        lhs = [operand(y, start), operand(y, start + chunk)]
        pred = lax.dot_general(
            jnp.concatenate(lhs, axis=0), rhs[...], (((0,), (0,)), ((), ())),
            preferred_element_type=f32,
        )
        return lhs, pred

    def misfit_of(y, b, pred):
        pieces, weight = [], None
        for j in range(2):
            at = pl.ds((2 * b + j) * chunk, chunk)
            w = wts[y, at].astype(f32)
            own = jnp.sum(w.reshape(chunk // 8, 8, dates), axis=0)
            weight = own if weight is None else weight + own
            mh, ml = split(w * (pred[:, j * dates : (j + 1) * dates] - obs[y, at].astype(f32)))
            both = jnp.concatenate([mh, ml], axis=1)
            misfits[y, at] = both
            pieces.append(both)
        return pieces, weight

    def gather(lhs, pieces):
        return sum(
            lax.dot_general(
                lhs[j][: 3 * rank], pieces[j], (((1,), (0,)), ((), ())),
                preferred_element_type=f32,
            )
            for j in range(2)
        )

    total = jnp.zeros((3 * rank, 2 * dates), f32)
    count = jnp.zeros((8, dates), f32)
    predicted = ready = None
    for step in range(rows * blocks + 2):
        y, b = divmod(step, blocks)
        for g, group in enumerate(groups):
            if b == 0 and y == group[0]:
                for row in group:
                    fac_copies[row].wait()
                    wts_copies[row].wait()
                    obs_copies[row].wait()
                fetch(g + 2)
        now = (y, b, *predict(y, b)) if y < rows else None
        if ready is not None:
            total = total + gather(*ready)
        ready = None
        if predicted is not None:
            py, pb_, lhs, pred = predicted
            pieces, weight = misfit_of(py, pb_, pred)
            count = count + weight
            ready = lhs, pieces
        predicted = now

    gdf = total[:rank, :dates] + total[:rank, dates:] + total[rank : 2 * rank, :dates]
    ones = 2 * rank + 2
    gdb = total[ones : ones + 1, :dates] + total[ones : ones + 1, dates:]
    parts[me] = jnp.concatenate(
        [gdf, gdb, jnp.sum(count, axis=0, keepdims=True)], axis=0
    )

    def send_part(peer):
        remote(parts.at[me], parts.at[me], part_sem.at[0], part_sem.at[1], peer).start()

    @pl.when(jnp.logical_not(is_root))
    def _():
        send_part(0)
        pl.semaphore_wait(go_sem, 1)

        def send_other(peer):
            @pl.when(peer != me)
            def _():
                send_part(peer)

        each_other(send_other)

    @pl.when(is_root)
    def _():
        pl.semaphore_wait(barrier, n - 1)
        each_other(
            lambda peer: pl.semaphore_signal(
                go_sem, inc=1, device_id={"space": peer}, device_id_type=pl.DeviceIdType.MESH
            )
        )
        greet()
        each_other(send_part)


    for y in range(rows):
        pix = lax.dot_general(
            back[...], misfits[y], (((1,), (1,)), ((), ())), preferred_element_type=f32
        )
        gpf_ref[y] = pix[:rank] + pix[rank : 2 * rank]
        gpb_ref[y : y + 1] = pix[2 * rank : 2 * rank + 1]

    def row_factors(y):
        return halo_f[0] if y < 0 else halo_f[1] if y == rows else fac[y]

    def smooth_row(y):
        own = cond[y + 1 : y + 2]
        north, south = cond[y : y + 1], cond[y + 2 : y + 3]
        f = fac[y]
        around = north + south + beside(own)
        weighted = north * row_factors(y - 1) + south * row_factors(y + 1) + beside(own * f)
        smooth[y] = own * (around * f - weighted)

    for y in range(1, rows - 1):
        smooth_row(y)

    @pl.when(is_root)
    def _():
        halo_f[0] = jnp.zeros((rank, cols), f32)
        halo_c[0] = jnp.zeros((1, cols), f32)

    @pl.when(jnp.logical_not(is_root))
    def _():
        halo[0].wait_send()
        halo[2].wait_send()
        halo[1].wait_recv()
        halo[3].wait_recv()

    @pl.when(is_last)
    def _():
        halo_f[1] = jnp.zeros((rank, cols), f32)
        halo_c[1] = jnp.zeros((1, cols), f32)

    @pl.when(jnp.logical_not(is_last))
    def _():
        halo[1].wait_send()
        halo[3].wait_send()
        halo[0].wait_recv()
        halo[2].wait_recv()

    cond[0:1] = halo_c[0]
    cond[rows + 1 : rows + 2] = halo_c[1]
    smooth_row(0)
    smooth_row(rows - 1)


    others = parts.at[pl.ds(0, n - 1)]
    wait_bytes(others, part_sem.at[1])
    whole = jnp.sum(parts[...], axis=0)
    clear = jnp.sum(whole[rank + 1 : rank + 2], axis=1, keepdims=True)
    scale = jnp.float32(n * rows * cols) / clear
    gdf_ref[...] = scale * whole[:rank]
    gdb_ref[...] = scale * whole[rank : rank + 1]
    gpb_ref[...] = scale * gpb_ref[...]
    for y in range(rows):
        gpf_ref[y] = scale * gpf_ref[y] + smooth[y]
    wait_bytes(others, part_sem.at[0])


def place(*refs):
    half = len(refs) // 2
    sem = refs[-1]
    copies = [
        pltpu.make_async_copy(refs[i], refs[half + i], sem.at[i]) for i in range(half)
    ]
    for copy in copies:
        copy.start()
    for copy in copies:
        copy.wait()


def on_device(
    observed, weights, pixel_factors, pixel_bias, date_factors, date_bias, land_class, conductance
):
    rows, rank, cols = pixel_factors.shape
    dates = observed.shape[2]
    n = lax.axis_size("space")
    f32, bf16 = jnp.float32, jnp.bfloat16
    dma = pltpu.SemaphoreType.DMA
    anywhere = pl.BlockSpec(memory_space=pl.ANY)
    vmem = pl.BlockSpec(memory_space=pltpu.VMEM)
    shapes = (
        jax.ShapeDtypeStruct((rows, rank, cols), f32),
        jax.ShapeDtypeStruct((rows, cols), f32),
        jax.ShapeDtypeStruct((rank, dates), f32),
        jax.ShapeDtypeStruct((1, dates), f32),
    )
    grads = pl.pallas_call(
        functools.partial(kernel, n, CHUNK),
        out_shape=tuple(pltpu.VMEM(x.shape, x.dtype) for x in shapes),
        in_specs=[anywhere] * 8,
        out_specs=(vmem,) * 4,
        scratch_shapes=[
            pltpu.SMEM((CLASSES,), f32),
            pltpu.VMEM((rank, dates), f32),
            pltpu.VMEM((1, dates), f32),
            pltpu.VMEM((rows, cols, dates), bf16),
            pltpu.VMEM((rows, cols, dates), bf16),
            pltpu.VMEM((rows, rank, cols), f32),
            pltpu.VMEM((rows, cols), f32),
            pltpu.VMEM((rows, cols), jnp.int32),
            pltpu.VMEM((rows, rank, cols), f32),
            pltpu.VMEM((2, rank, cols), f32),
            pltpu.VMEM((2, 1, cols), f32),
            pltpu.VMEM((2, 1, cols), f32),
            pltpu.VMEM((128, 2 * dates), bf16),
            pltpu.VMEM((48, 2 * dates), bf16),
            pltpu.VMEM((rows, cols, 2 * dates), bf16),
            pltpu.VMEM((n, 18, dates), f32),
            pltpu.VMEM((rows + 2, cols), f32),
            dma((rows,)), dma((rows,)), dma((rows,)), dma((5,)),
            dma((4,)), dma((4,)), dma((2,)),
            pltpu.SemaphoreType.REGULAR,
        ],
        compiler_params=pltpu.CompilerParams(
            collective_id=0, has_side_effects=True, vmem_limit_bytes=GRANT
        ),
        name="gap_fill",
    )(
        *(
            pltpu.with_memory_space_constraint(x, pltpu.HBM)
            for x in (
                conductance, observed, weights, pixel_factors, pixel_bias, date_factors,
                date_bias.reshape(1, dates), land_class,
            )
        )
    )
    gpf, gpb, gdf, gdb = pl.pallas_call(
        place,
        out_shape=shapes,
        in_specs=[vmem] * 4,
        out_specs=(anywhere,) * 4,
        scratch_shapes=[dma((4,))],
        compiler_params=pltpu.CompilerParams(vmem_limit_bytes=4 * 1024 * 1024),
        name="place",
    )(*grads)
    return gpf, gpb, gdf, gdb.reshape(dates)


def solution(mesh):
    return jax.shard_map(
        on_device,
        mesh=mesh,
        in_specs=(
            P(("parts", "space"), None, None),
            P(("parts", "space"), None, None),
            P(("parts", "space"), None, None),
            P(("parts", "space"), None),
            P("parts", None),
            P("parts"),
            P(("parts", "space"), None),
            P(),
        ),
        out_specs=(
            P(("parts", "space"), None, None),
            P(("parts", "space"), None),
            P("parts", None),
            P("parts"),
        ),
        check_vma=False,
    )
```

```python
import functools

import jax
import jax.numpy as jnp
from jax import lax
from jax.experimental import pallas as pl
from jax.experimental.pallas import tpu as pltpu
from jax.sharding import PartitionSpec as P

CLASSES = 4
CHUNK = 256
GRANT = 44 * 1024 * 1024


def split(x):
    head = x.astype(jnp.bfloat16)
    return head, (x - head.astype(jnp.float32)).astype(jnp.bfloat16)


def lookup(land_class, cond_ref):
    cond = jnp.zeros(land_class.shape, jnp.float32)
    for klass in range(CLASSES):
        cond = cond + jnp.where(land_class == klass, cond_ref[klass], jnp.float32(0.0))
    return cond


def beside(x):
    cols = x.shape[1]
    col = lax.broadcasted_iota(jnp.int32, x.shape, 1)
    left = jnp.where(col == 0, 0.0, pltpu.roll(x, 1, 1))
    right = jnp.where(col == cols - 1, 0.0, pltpu.roll(x, cols - 1, 1))
    return left + right


def kernel(
    n, chunk,
    cond_hbm, obs_hbm, wts_hbm, fac_hbm, pb_hbm, df_hbm, db_hbm, lc_hbm,
    gpf_ref, gpb_ref, smooth, whole_ref,
    cond_ref, df_ref, db_ref,
    obs, wts, fac, pb, lc, halo_f, halo_c, edge_c, rhs, back, misfits, parts, cond,
    obs_sem, wts_sem, fac_sem, small_sem,
    halo_send, halo_recv, part_sem, go_sem,
):
    rows, rank, cols = fac.shape
    dates = obs.shape[2]
    f32, bf16 = jnp.float32, jnp.bfloat16

    me = lax.axis_index("space")
    above, below = jnp.maximum(me - 1, 0), jnp.minimum(me + 1, n - 1)

    def signal(peer):
        pl.semaphore_signal(
            barrier, inc=1, device_id={"space": peer}, device_id_type=pl.DeviceIdType.MESH
        )

    def each_other(act):
        if n <= 32:
            for peer in range(1, n):
                act(peer)
        else:
            lax.fori_loop(1, n, lambda peer, none: (act(peer), none)[1], 0)

    barrier = pltpu.get_barrier_semaphore()
    is_root, is_last = me == 0, me == n - 1

    df_copy = pltpu.make_async_copy(df_hbm, df_ref, small_sem.at[2])
    db_copy = pltpu.make_async_copy(db_hbm, db_ref, small_sem.at[3])
    cond_copy = pltpu.make_async_copy(cond_hbm, cond_ref, small_sem.at[4])
    pb_copy = pltpu.make_async_copy(pb_hbm, pb, small_sem.at[0])
    lc_copy = pltpu.make_async_copy(lc_hbm, lc, small_sem.at[1])
    fac_copies = [
        pltpu.make_async_copy(fac_hbm.at[y], fac.at[y], fac_sem.at[y]) for y in range(rows)
    ]
    obs_copies = [
        pltpu.make_async_copy(obs_hbm.at[y], obs.at[y], obs_sem.at[y]) for y in range(rows)
    ]
    wts_copies = [
        pltpu.make_async_copy(wts_hbm.at[y], wts.at[y], wts_sem.at[y]) for y in range(rows)
    ]
    cond_copy.start()
    lc_copy.start()
    df_copy.start()
    db_copy.start()
    pb_copy.start()
    groups = [[0], [1], [2], [3]]

    def fetch(g):
        if g < len(groups):
            for y in groups[g]:
                fac_copies[y].start()
                wts_copies[y].start()
                obs_copies[y].start()

    for g in range(1):
        fetch(g)

    @pl.when(is_root)
    def _():
        each_other(signal)

    @pl.when(jnp.logical_not(is_root))
    def _():
        signal(0)

        @pl.when(me > 1)
        def _():
            signal(above)

        @pl.when(jnp.logical_not(is_last))
        def _():
            signal(below)

    df_copy.wait()
    db_copy.wait()
    dh, dl = split(df_ref[...])
    bh, bl = split(db_ref[...])
    line = lax.broadcasted_iota(jnp.int32, (16, dates), 0)
    tail = jnp.where(
        line < 2, 1.0,
        jnp.where(line == 2, bh.astype(f32), jnp.where(line == 3, bl.astype(f32), 0.0)),
    ).astype(bf16)
    one = jnp.concatenate([dh, dh, tail, dl], axis=0)
    none = jnp.zeros_like(one)
    rhs[...] = jnp.concatenate(
        [jnp.concatenate([one, none], axis=1), jnp.concatenate([none, one], axis=1)], axis=0
    )
    ones_line = jnp.where(line == 0, 1.0, 0.0).astype(bf16)
    back[...] = jnp.concatenate(
        [
            jnp.concatenate([dh, dh], axis=1),
            jnp.concatenate([dl, jnp.zeros_like(dl)], axis=1),
            jnp.concatenate([ones_line, ones_line], axis=1),
        ],
        axis=0,
    )

    def remote(src, dst, send, recv, peer):
        return pltpu.make_async_remote_copy(
            src_ref=src, dst_ref=dst, send_sem=send, recv_sem=recv,
            device_id={"space": peer}, device_id_type=pl.DeviceIdType.MESH,
        )

    def wait_bytes(ref, sem):
        pltpu.make_async_copy(ref, ref, sem).wait()

    halo = [
        remote(fac_hbm.at[0], halo_f.at[1], halo_send.at[0], halo_recv.at[0], above),
        remote(fac_hbm.at[rows - 1], halo_f.at[0], halo_send.at[1], halo_recv.at[1], below),
        remote(edge_c.at[0], halo_c.at[1], halo_send.at[2], halo_recv.at[2], above),
        remote(edge_c.at[1], halo_c.at[0], halo_send.at[3], halo_recv.at[3], below),
    ]
    pb_copy.wait()

    def greet():
        lc_copy.wait()
        cond_copy.wait()
        cond[1 : rows + 1] = lookup(lc[...], cond_ref)
        edge_c[0] = cond[1:2]
        edge_c[1] = cond[rows : rows + 1]


        @pl.when(jnp.logical_not(is_root))
        def _():
            halo[0].start()
            halo[2].start()

        @pl.when(jnp.logical_not(is_last))
        def _():
            halo[1].start()
            halo[3].start()

    slot = lax.broadcasted_iota(jnp.int32, (16, chunk), 0)

    def operand(y, start):
        at = pl.ds(start, chunk)
        fh, fl = split(fac[y, :, at])
        ph, plow = split(pb[y : y + 1, at])
        extra = jnp.where(
            slot == 0, ph.astype(f32),
            jnp.where(slot == 1, plow.astype(f32), jnp.where(slot < 4, 1.0, 0.0)),
        ).astype(bf16)
        return jnp.concatenate([fh, fl, extra, fh], axis=0)

    for g in range(1, 2):
        fetch(g)

    @pl.when(jnp.logical_not(is_root))
    def _():
        pl.semaphore_wait(
            barrier, 3 - (me == 1).astype(jnp.int32) - is_last.astype(jnp.int32)
        )
        greet()

    blocks = cols // (2 * chunk)
    def predict(y, b):
        start = b * 2 * chunk
        lhs = [operand(y, start), operand(y, start + chunk)]
        pred = lax.dot_general(
            jnp.concatenate(lhs, axis=0), rhs[...], (((0,), (0,)), ((), ())),
            preferred_element_type=f32,
        )
        return lhs, pred

    def misfit_of(y, b, pred):
        pieces, weight = [], None
        for j in range(2):
            at = pl.ds((2 * b + j) * chunk, chunk)
            w = wts[y, at].astype(f32)
            own = jnp.sum(w.reshape(chunk // 8, 8, dates), axis=0)
            weight = own if weight is None else weight + own
            mh, ml = split(w * (pred[:, j * dates : (j + 1) * dates] - obs[y, at].astype(f32)))
            both = jnp.concatenate([mh, ml], axis=1)
            misfits[y, at] = both
            pieces.append(both)
        return pieces, weight

    def gather(lhs, pieces):
        return sum(
            lax.dot_general(
                lhs[j][: 3 * rank], pieces[j], (((1,), (0,)), ((), ())),
                preferred_element_type=f32,
            )
            for j in range(2)
        )

    total = jnp.zeros((3 * rank, 2 * dates), f32)
    count = jnp.zeros((8, dates), f32)
    predicted = ready = None
    for step in range(rows * blocks + 2):
        y, b = divmod(step, blocks)
        for g, group in enumerate(groups):
            if b == 0 and y == group[0]:
                for row in group:
                    fac_copies[row].wait()
                    wts_copies[row].wait()
                    obs_copies[row].wait()
                fetch(g + 2)
        now = (y, b, *predict(y, b)) if y < rows else None
        if ready is not None:
            total = total + gather(*ready)
        ready = None
        if predicted is not None:
            py, pb_, lhs, pred = predicted
            pieces, weight = misfit_of(py, pb_, pred)
            count = count + weight
            ready = lhs, pieces
        predicted = now

    gdf = total[:rank, :dates] + total[:rank, dates:] + total[rank : 2 * rank, :dates]
    ones = 2 * rank + 2
    gdb = total[ones : ones + 1, :dates] + total[ones : ones + 1, dates:]
    parts[me] = jnp.concatenate(
        [gdf, gdb, jnp.sum(count, axis=0, keepdims=True)], axis=0
    )

    def send_part(peer):
        remote(parts.at[me], parts.at[me], part_sem.at[0], part_sem.at[1], peer).start()

    @pl.when(jnp.logical_not(is_root))
    def _():
        send_part(0)
        pl.semaphore_wait(go_sem, 1)

        def send_other(peer):
            @pl.when(peer != me)
            def _():
                send_part(peer)

        each_other(send_other)

    @pl.when(is_root)
    def _():
        pl.semaphore_wait(barrier, n - 1)
        each_other(
            lambda peer: pl.semaphore_signal(
                go_sem, inc=1, device_id={"space": peer}, device_id_type=pl.DeviceIdType.MESH
            )
        )
        greet()
        each_other(send_part)


    for y in range(rows):
        pix = lax.dot_general(
            back[...], misfits[y], (((1,), (1,)), ((), ())), preferred_element_type=f32
        )
        gpf_ref[y] = pix[:rank] + pix[rank : 2 * rank]
        gpb_ref[y : y + 1] = pix[2 * rank : 2 * rank + 1]

    def row_factors(y):
        return halo_f[0] if y < 0 else halo_f[1] if y == rows else fac[y]

    def smooth_row(y):
        own = cond[y + 1 : y + 2]
        north, south = cond[y : y + 1], cond[y + 2 : y + 3]
        f = fac[y]
        around = north + south + beside(own)
        weighted = north * row_factors(y - 1) + south * row_factors(y + 1) + beside(own * f)
        smooth[y] = own * (around * f - weighted)

    for y in range(1, rows - 1):
        smooth_row(y)

    @pl.when(is_root)
    def _():
        halo_f[0] = jnp.zeros((rank, cols), f32)
        halo_c[0] = jnp.zeros((1, cols), f32)

    @pl.when(jnp.logical_not(is_root))
    def _():
        halo[0].wait_send()
        halo[2].wait_send()
        halo[1].wait_recv()
        halo[3].wait_recv()

    @pl.when(is_last)
    def _():
        halo_f[1] = jnp.zeros((rank, cols), f32)
        halo_c[1] = jnp.zeros((1, cols), f32)

    @pl.when(jnp.logical_not(is_last))
    def _():
        halo[1].wait_send()
        halo[3].wait_send()
        halo[0].wait_recv()
        halo[2].wait_recv()

    cond[0:1] = halo_c[0]
    cond[rows + 1 : rows + 2] = halo_c[1]
    smooth_row(0)
    smooth_row(rows - 1)


    others = parts.at[pl.ds(0, n - 1)]
    wait_bytes(others, part_sem.at[0])
    wait_bytes(others, part_sem.at[1])
    whole = jnp.sum(parts[...], axis=0)
    whole_ref[...] = whole


def place(
    pixels,
    pix_ref, pixb_ref, smooth_ref, whole_ref, gpf_hbm, gpb_hbm, gdf_hbm, gdb_hbm,
    gpf, gpb, gdf, gdb, sem,
):
    rows, rank, _ = gpf.shape
    clear = jnp.sum(whole_ref[rank + 1 : rank + 2], axis=1, keepdims=True)
    scale = jnp.float32(pixels) / clear
    copies = []

    def send(src, dst):
        copies.append(pltpu.make_async_copy(src, dst, sem.at[len(copies)]))
        copies[-1].start()

    for y in range(rows):
        gpf[y] = scale * pix_ref[y] + smooth_ref[y]
        send(gpf.at[y], gpf_hbm.at[y])
    gpb[...] = scale * pixb_ref[...]
    send(gpb, gpb_hbm)
    gdf[...] = scale * whole_ref[:rank]
    send(gdf, gdf_hbm)
    gdb[...] = scale * whole_ref[rank : rank + 1]
    send(gdb, gdb_hbm)
    for copy in copies:
        copy.wait()


def on_device(
    observed, weights, pixel_factors, pixel_bias, date_factors, date_bias, land_class, conductance
):
    rows, rank, cols = pixel_factors.shape
    dates = observed.shape[2]
    n = lax.axis_size("space")
    f32, bf16 = jnp.float32, jnp.bfloat16
    dma = pltpu.SemaphoreType.DMA
    anywhere = pl.BlockSpec(memory_space=pl.ANY)
    vmem = pl.BlockSpec(memory_space=pltpu.VMEM)
    shapes = (
        jax.ShapeDtypeStruct((rows, rank, cols), f32),
        jax.ShapeDtypeStruct((rows, cols), f32),
        jax.ShapeDtypeStruct((rank, dates), f32),
        jax.ShapeDtypeStruct((1, dates), f32),
    )
    grads = pl.pallas_call(
        functools.partial(kernel, n, CHUNK),
        out_shape=tuple(
            pltpu.VMEM(shape, f32)
            for shape in (shapes[0].shape, shapes[1].shape, shapes[0].shape, (18, dates))
        ),
        in_specs=[anywhere] * 8,
        out_specs=(vmem,) * 4,
        scratch_shapes=[
            pltpu.SMEM((CLASSES,), f32),
            pltpu.VMEM((rank, dates), f32),
            pltpu.VMEM((1, dates), f32),
            pltpu.VMEM((rows, cols, dates), bf16),
            pltpu.VMEM((rows, cols, dates), bf16),
            pltpu.VMEM((rows, rank, cols), f32),
            pltpu.VMEM((rows, cols), f32),
            pltpu.VMEM((rows, cols), jnp.int32),
            pltpu.VMEM((2, rank, cols), f32),
            pltpu.VMEM((2, 1, cols), f32),
            pltpu.VMEM((2, 1, cols), f32),
            pltpu.VMEM((128, 2 * dates), bf16),
            pltpu.VMEM((48, 2 * dates), bf16),
            pltpu.VMEM((rows, cols, 2 * dates), bf16),
            pltpu.VMEM((n, 18, dates), f32),
            pltpu.VMEM((rows + 2, cols), f32),
            dma((rows,)), dma((rows,)), dma((rows,)), dma((5,)),
            dma((4,)), dma((4,)), dma((2,)),
            pltpu.SemaphoreType.REGULAR,
        ],
        compiler_params=pltpu.CompilerParams(
            collective_id=0, has_side_effects=True, vmem_limit_bytes=GRANT
        ),
        name="gap_fill",
    )(
        *(
            pltpu.with_memory_space_constraint(x, pltpu.HBM)
            for x in (
                conductance, observed, weights, pixel_factors, pixel_bias, date_factors,
                date_bias.reshape(1, dates), land_class,
            )
        )
    )
    gpf, gpb, gdf, gdb = pl.pallas_call(
        functools.partial(place, n * rows * cols),
        out_shape=shapes,
        in_specs=[vmem] * 4,
        out_specs=(anywhere,) * 4,
        scratch_shapes=[pltpu.VMEM(x.shape, f32) for x in shapes] + [dma((rows + 3,))],
        compiler_params=pltpu.CompilerParams(vmem_limit_bytes=4 * 1024 * 1024),
        name="place",
    )(*grads)
    return gpf, gpb, gdf, gdb.reshape(dates)


def solution(mesh):
    return jax.shard_map(
        on_device,
        mesh=mesh,
        in_specs=(
            P(("parts", "space"), None, None),
            P(("parts", "space"), None, None),
            P(("parts", "space"), None, None),
            P(("parts", "space"), None),
            P("parts", None),
            P("parts"),
            P(("parts", "space"), None),
            P(),
        ),
        out_specs=(
            P(("parts", "space"), None, None),
            P(("parts", "space"), None),
            P("parts", None),
            P("parts"),
        ),
        check_vma=False,
    )
```

```python
import functools

import jax
import jax.numpy as jnp
from jax import lax
from jax.experimental import pallas as pl
from jax.experimental.pallas import tpu as pltpu
from jax.sharding import PartitionSpec as P

CLASSES = 4
CHUNK = 256
GRANT = 44 * 1024 * 1024


def split(x):
    head = x.astype(jnp.bfloat16)
    return head, (x - head.astype(jnp.float32)).astype(jnp.bfloat16)


def lookup(land_class, cond_ref):
    cond = jnp.zeros(land_class.shape, jnp.float32)
    for klass in range(CLASSES):
        cond = cond + jnp.where(land_class == klass, cond_ref[klass], jnp.float32(0.0))
    return cond


def beside(x):
    cols = x.shape[1]
    col = lax.broadcasted_iota(jnp.int32, x.shape, 1)
    left = jnp.where(col == 0, 0.0, pltpu.roll(x, 1, 1))
    right = jnp.where(col == cols - 1, 0.0, pltpu.roll(x, cols - 1, 1))
    return left + right


def kernel(
    n, chunk,
    cond_hbm, obs_hbm, wts_hbm, fac_hbm, pb_hbm, df_hbm, db_hbm, lc_hbm,
    gpf_ref, gpb_ref, smooth, whole_ref,
    cond_ref, df_ref, db_ref,
    obs, wts, fac, pb, lc, halo_f, halo_c, edge_c, rhs, back, misfits, parts, cond,
    obs_sem, wts_sem, fac_sem, small_sem,
    halo_send, halo_recv, part_sem, go_sem,
):
    rows, rank, cols = fac.shape
    dates = obs.shape[2]
    f32, bf16 = jnp.float32, jnp.bfloat16

    me = lax.axis_index("space")
    above, below = jnp.maximum(me - 1, 0), jnp.minimum(me + 1, n - 1)

    def signal(peer):
        pl.semaphore_signal(
            barrier, inc=1, device_id={"space": peer}, device_id_type=pl.DeviceIdType.MESH
        )

    def each_other(act):
        if n <= 32:
            for peer in range(1, n):
                act(peer)
        else:
            lax.fori_loop(1, n, lambda peer, none: (act(peer), none)[1], 0)

    barrier = pltpu.get_barrier_semaphore()
    is_root, is_last = me == 0, me == n - 1

    df_copy = pltpu.make_async_copy(df_hbm, df_ref, small_sem.at[2])
    db_copy = pltpu.make_async_copy(db_hbm, db_ref, small_sem.at[3])
    cond_copy = pltpu.make_async_copy(cond_hbm, cond_ref, small_sem.at[4])
    pb_copy = pltpu.make_async_copy(pb_hbm, pb, small_sem.at[0])
    lc_copy = pltpu.make_async_copy(lc_hbm, lc, small_sem.at[1])
    fac_copies = [
        pltpu.make_async_copy(fac_hbm.at[y], fac.at[y], fac_sem.at[y]) for y in range(rows)
    ]
    obs_copies = [
        pltpu.make_async_copy(obs_hbm.at[y], obs.at[y], obs_sem.at[y]) for y in range(rows)
    ]
    wts_copies = [
        pltpu.make_async_copy(wts_hbm.at[y], wts.at[y], wts_sem.at[y]) for y in range(rows)
    ]
    df_copy.start()
    db_copy.start()
    cond_copy.start()
    lc_copy.start()
    pb_copy.start()
    groups = [[0], [1], [2], [3]]

    def fetch(g):
        if g < len(groups):
            for y in groups[g]:
                fac_copies[y].start()
                wts_copies[y].start()
                obs_copies[y].start()

    for g in range(1):
        fetch(g)

    @pl.when(is_root)
    def _():
        each_other(signal)

    @pl.when(jnp.logical_not(is_root))
    def _():
        signal(0)

        @pl.when(me > 1)
        def _():
            signal(above)

        @pl.when(jnp.logical_not(is_last))
        def _():
            signal(below)

    df_copy.wait()
    db_copy.wait()
    dh, dl = split(df_ref[...])
    bh, bl = split(db_ref[...])
    line = lax.broadcasted_iota(jnp.int32, (16, dates), 0)
    tail = jnp.where(
        line < 2, 1.0,
        jnp.where(line == 2, bh.astype(f32), jnp.where(line == 3, bl.astype(f32), 0.0)),
    ).astype(bf16)
    one = jnp.concatenate([dh, dh, tail, dl], axis=0)
    none = jnp.zeros_like(one)
    rhs[...] = jnp.concatenate(
        [jnp.concatenate([one, none], axis=1), jnp.concatenate([none, one], axis=1)], axis=0
    )
    ones_line = jnp.where(line == 0, 1.0, 0.0).astype(bf16)
    back[...] = jnp.concatenate(
        [
            jnp.concatenate([dh, dh], axis=1),
            jnp.concatenate([dl, jnp.zeros_like(dl)], axis=1),
            jnp.concatenate([ones_line, ones_line], axis=1),
        ],
        axis=0,
    )

    def remote(src, dst, send, recv, peer):
        return pltpu.make_async_remote_copy(
            src_ref=src, dst_ref=dst, send_sem=send, recv_sem=recv,
            device_id={"space": peer}, device_id_type=pl.DeviceIdType.MESH,
        )

    def wait_bytes(ref, sem):
        pltpu.make_async_copy(ref, ref, sem).wait()

    halo = [
        remote(fac_hbm.at[0], halo_f.at[1], halo_send.at[0], halo_recv.at[0], above),
        remote(fac_hbm.at[rows - 1], halo_f.at[0], halo_send.at[1], halo_recv.at[1], below),
        remote(edge_c.at[0], halo_c.at[1], halo_send.at[2], halo_recv.at[2], above),
        remote(edge_c.at[1], halo_c.at[0], halo_send.at[3], halo_recv.at[3], below),
    ]
    pb_copy.wait()

    def greet():
        lc_copy.wait()
        cond_copy.wait()
        cond[1 : rows + 1] = lookup(lc[...], cond_ref)
        edge_c[0] = cond[1:2]
        edge_c[1] = cond[rows : rows + 1]


        @pl.when(jnp.logical_not(is_root))
        def _():
            halo[0].start()
            halo[2].start()

        @pl.when(jnp.logical_not(is_last))
        def _():
            halo[1].start()
            halo[3].start()

    slot = lax.broadcasted_iota(jnp.int32, (16, chunk), 0)

    def operand(y, start):
        at = pl.ds(start, chunk)
        fh, fl = split(fac[y, :, at])
        ph, plow = split(pb[y : y + 1, at])
        extra = jnp.where(
            slot == 0, ph.astype(f32),
            jnp.where(slot == 1, plow.astype(f32), jnp.where(slot < 4, 1.0, 0.0)),
        ).astype(bf16)
        return jnp.concatenate([fh, fl, extra, fh], axis=0)

    for g in range(1, 2):
        fetch(g)

    @pl.when(jnp.logical_not(is_root))
    def _():
        pl.semaphore_wait(
            barrier, 3 - (me == 1).astype(jnp.int32) - is_last.astype(jnp.int32)
        )
        greet()

    blocks = cols // (2 * chunk)
    def predict(y, b):
        start = b * 2 * chunk
        lhs = [operand(y, start), operand(y, start + chunk)]
        pred = lax.dot_general(
            jnp.concatenate(lhs, axis=0), rhs[...], (((0,), (0,)), ((), ())),
            preferred_element_type=f32,
        )
        return lhs, pred

    def misfit_of(y, b, pred):
        pieces, weight = [], None
        for j in range(2):
            at = pl.ds((2 * b + j) * chunk, chunk)
            w = wts[y, at].astype(f32)
            own = jnp.sum(w.reshape(chunk // 8, 8, dates), axis=0)
            weight = own if weight is None else weight + own
            mh, ml = split(w * (pred[:, j * dates : (j + 1) * dates] - obs[y, at].astype(f32)))
            both = jnp.concatenate([mh, ml], axis=1)
            misfits[y, at] = both
            pieces.append(both)
        return pieces, weight

    def gather(lhs, pieces):
        return sum(
            lax.dot_general(
                lhs[j][: 3 * rank], pieces[j], (((1,), (0,)), ((), ())),
                preferred_element_type=f32,
            )
            for j in range(2)
        )

    total = jnp.zeros((3 * rank, 2 * dates), f32)
    count = jnp.zeros((8, dates), f32)
    predicted = ready = None
    for step in range(rows * blocks + 2):
        y, b = divmod(step, blocks)
        for g, group in enumerate(groups):
            if b == 0 and y == group[0]:
                for row in group:
                    fac_copies[row].wait()
                    wts_copies[row].wait()
                    obs_copies[row].wait()
                fetch(g + 2)
        now = (y, b, *predict(y, b)) if y < rows else None
        if ready is not None:
            total = total + gather(*ready)
        ready = None
        if predicted is not None:
            py, pb_, lhs, pred = predicted
            pieces, weight = misfit_of(py, pb_, pred)
            count = count + weight
            ready = lhs, pieces
        predicted = now

    gdf = total[:rank, :dates] + total[:rank, dates:] + total[rank : 2 * rank, :dates]
    ones = 2 * rank + 2
    gdb = total[ones : ones + 1, :dates] + total[ones : ones + 1, dates:]
    parts[me] = jnp.concatenate(
        [gdf, gdb, jnp.sum(count, axis=0, keepdims=True)], axis=0
    )

    def send_part(peer):
        remote(parts.at[me], parts.at[me], part_sem.at[0], part_sem.at[1], peer).start()

    @pl.when(jnp.logical_not(is_root))
    def _():
        send_part(0)
        pl.semaphore_wait(go_sem, 1)

        def send_other(peer):
            @pl.when(peer != me)
            def _():
                send_part(peer)

        each_other(send_other)

    @pl.when(is_root)
    def _():
        pl.semaphore_wait(barrier, n - 1)
        each_other(
            lambda peer: pl.semaphore_signal(
                go_sem, inc=1, device_id={"space": peer}, device_id_type=pl.DeviceIdType.MESH
            )
        )
        greet()
        each_other(send_part)


    for y in range(rows):
        pix = lax.dot_general(
            back[...], misfits[y], (((1,), (1,)), ((), ())), preferred_element_type=f32
        )
        gpf_ref[y] = pix[:rank] + pix[rank : 2 * rank]
        gpb_ref[y : y + 1] = pix[2 * rank : 2 * rank + 1]

    def row_factors(y):
        return halo_f[0] if y < 0 else halo_f[1] if y == rows else fac[y]

    def smooth_row(y):
        own = cond[y + 1 : y + 2]
        north, south = cond[y : y + 1], cond[y + 2 : y + 3]
        f = fac[y]
        around = north + south + beside(own)
        weighted = north * row_factors(y - 1) + south * row_factors(y + 1) + beside(own * f)
        smooth[y] = own * (around * f - weighted)

    for y in range(1, rows - 1):
        smooth_row(y)

    @pl.when(is_root)
    def _():
        halo_f[0] = jnp.zeros((rank, cols), f32)
        halo_c[0] = jnp.zeros((1, cols), f32)

    @pl.when(jnp.logical_not(is_root))
    def _():
        halo[0].wait_send()
        halo[2].wait_send()
        halo[1].wait_recv()
        halo[3].wait_recv()

    @pl.when(is_last)
    def _():
        halo_f[1] = jnp.zeros((rank, cols), f32)
        halo_c[1] = jnp.zeros((1, cols), f32)

    @pl.when(jnp.logical_not(is_last))
    def _():
        halo[1].wait_send()
        halo[3].wait_send()
        halo[0].wait_recv()
        halo[2].wait_recv()

    cond[0:1] = halo_c[0]
    cond[rows + 1 : rows + 2] = halo_c[1]
    smooth_row(0)
    smooth_row(rows - 1)


    others = parts.at[pl.ds(0, n - 1)]
    wait_bytes(others, part_sem.at[0])
    wait_bytes(others, part_sem.at[1])
    whole = jnp.sum(parts[...], axis=0)
    whole_ref[...] = whole


def place(
    pixels,
    pix_ref, pixb_ref, smooth_ref, whole_ref, gpf_hbm, gpb_hbm, gdf_hbm, gdb_hbm,
    gpf, gpb, gdf, gdb, sem,
):
    rows, rank, _ = gpf.shape
    clear = jnp.sum(whole_ref[rank + 1 : rank + 2], axis=1, keepdims=True)
    scale = jnp.float32(pixels) / clear
    copies = []

    def send(src, dst):
        copies.append(pltpu.make_async_copy(src, dst, sem.at[len(copies)]))
        copies[-1].start()

    for y in range(rows):
        gpf[y] = scale * pix_ref[y] + smooth_ref[y]
        send(gpf.at[y], gpf_hbm.at[y])
    gpb[...] = scale * pixb_ref[...]
    send(gpb, gpb_hbm)
    gdf[...] = scale * whole_ref[:rank]
    send(gdf, gdf_hbm)
    gdb[...] = scale * whole_ref[rank : rank + 1]
    send(gdb, gdb_hbm)
    for copy in copies:
        copy.wait()


def on_device(
    observed, weights, pixel_factors, pixel_bias, date_factors, date_bias, land_class, conductance
):
    rows, rank, cols = pixel_factors.shape
    dates = observed.shape[2]
    n = lax.axis_size("space")
    f32, bf16 = jnp.float32, jnp.bfloat16
    dma = pltpu.SemaphoreType.DMA
    anywhere = pl.BlockSpec(memory_space=pl.ANY)
    vmem = pl.BlockSpec(memory_space=pltpu.VMEM)
    shapes = (
        jax.ShapeDtypeStruct((rows, rank, cols), f32),
        jax.ShapeDtypeStruct((rows, cols), f32),
        jax.ShapeDtypeStruct((rank, dates), f32),
        jax.ShapeDtypeStruct((1, dates), f32),
    )
    grads = pl.pallas_call(
        functools.partial(kernel, n, CHUNK),
        out_shape=tuple(
            pltpu.VMEM(shape, f32)
            for shape in (shapes[0].shape, shapes[1].shape, shapes[0].shape, (18, dates))
        ),
        in_specs=[anywhere] * 8,
        out_specs=(vmem,) * 4,
        scratch_shapes=[
            pltpu.SMEM((CLASSES,), f32),
            pltpu.VMEM((rank, dates), f32),
            pltpu.VMEM((1, dates), f32),
            pltpu.VMEM((rows, cols, dates), bf16),
            pltpu.VMEM((rows, cols, dates), bf16),
            pltpu.VMEM((rows, rank, cols), f32),
            pltpu.VMEM((rows, cols), f32),
            pltpu.VMEM((rows, cols), jnp.int32),
            pltpu.VMEM((2, rank, cols), f32),
            pltpu.VMEM((2, 1, cols), f32),
            pltpu.VMEM((2, 1, cols), f32),
            pltpu.VMEM((128, 2 * dates), bf16),
            pltpu.VMEM((48, 2 * dates), bf16),
            pltpu.VMEM((rows, cols, 2 * dates), bf16),
            pltpu.VMEM((n, 18, dates), f32),
            pltpu.VMEM((rows + 2, cols), f32),
            dma((rows,)), dma((rows,)), dma((rows,)), dma((5,)),
            dma((4,)), dma((4,)), dma((2,)),
            pltpu.SemaphoreType.REGULAR,
        ],
        compiler_params=pltpu.CompilerParams(
            collective_id=0, has_side_effects=True, vmem_limit_bytes=GRANT
        ),
        name="gap_fill",
    )(
        *(
            pltpu.with_memory_space_constraint(x, pltpu.HBM)
            for x in (
                conductance, observed, weights, pixel_factors, pixel_bias, date_factors,
                date_bias.reshape(1, dates), land_class,
            )
        )
    )
    gpf, gpb, gdf, gdb = pl.pallas_call(
        functools.partial(place, n * rows * cols),
        out_shape=shapes,
        in_specs=[vmem] * 4,
        out_specs=(anywhere,) * 4,
        scratch_shapes=[pltpu.VMEM(x.shape, f32) for x in shapes] + [dma((rows + 3,))],
        compiler_params=pltpu.CompilerParams(vmem_limit_bytes=4 * 1024 * 1024),
        name="place",
    )(*grads)
    return gpf, gpb, gdf, gdb.reshape(dates)


def solution(mesh):
    return jax.shard_map(
        on_device,
        mesh=mesh,
        in_specs=(
            P(("parts", "space"), None, None),
            P(("parts", "space"), None, None),
            P(("parts", "space"), None, None),
            P(("parts", "space"), None),
            P("parts", None),
            P("parts"),
            P(("parts", "space"), None),
            P(),
        ),
        out_specs=(
            P(("parts", "space"), None, None),
            P(("parts", "space"), None),
            P("parts", None),
            P("parts"),
        ),
        check_vma=False,
    )
```
